128 devices in a mesh: fold: 4 (over x_hi, core), tile: 32 (over y, x_lo, z).
Axes of the slice: x: 4 (x_hi: 2, x_lo: 2; x = x_hi * 2 + x_lo), y: 4, z: 4, core: 2. Of those that a mesh axis runs over, the one named last changes fastest.
Arguments:
- design: bfloat16 [8192, 8192], P('fold', 'tile'), may hold values from -0.0625 to 0.0625
- weights: float32 [8192], P('fold'), may hold values from 0.2 to 5
- response: float32 [8192], P('fold'), may hold values from -6 to 6
- fold_of: int32 [32], P('fold'), may hold values from 0 to 7, as said below
- smoothing: float32 [128], P('tile'), may hold values from 0.05 to 1
Outputs:
- complement: float32 [8, 8192, 8192], P('fold', 'tile')
- complement_rhs: float32 [8, 8192], P('fold', 'tile')
The draws below stay inside these ranges and needn't reach their ends.
Inputs may be any that keep to these rules, and one draw needn't show every extreme that they name: `fold_of`: the slabs of rows g * 2048 to (g + 1) * 2048 - 1 carry only fold ids g * 2 to (g + 1) * 2 - 1, and each of these appears on at least one of those slabs.
All inputs are finite; a program needn't handle non-finite values.
Results may differ from the reference program's by a relative error of at most 0.0029.
Values may be sent and summed in bfloat16 or wider, within the bound.
No kernel may reach another device: no remote copies, remote signals or barrier semaphores. Data moves between devices by JAX's collectives and lax.ppermute only.
A program may use at most 256 MiB of HBM per device.

```python
import math
import jax
import jax.numpy as jnp
from jax import lax

P_SIZE = 8192
FOLDS = 8
TERM = 64
SLAB = 256
ROWS_DEV = 2048
ROWS = 8192
TERMS = 128


def draw_fold_of(key, part):
    per_group = ROWS_DEV // SLAB
    groups = ROWS // ROWS_DEV
    per_fold = FOLDS // groups
    scores = jax.random.randint(jax.random.fold_in(key, 11), (groups, per_group), 0, 1 << 20).astype(jnp.int32)
    scores = scores * per_group + jnp.arange(per_group, dtype=jnp.int32)[None, :]
    ranks = jnp.argsort(jnp.argsort(scores, axis=1, stable=True), axis=1, stable=True).astype(jnp.int32)
    extra = jax.random.randint(jax.random.fold_in(key, 12), (groups, per_group), 0, per_fold).astype(jnp.int32)
    local_id = jnp.where(ranks < per_fold, ranks, extra)
    folds = jnp.arange(groups, dtype=jnp.int32)[:, None] * per_fold + local_id
    return folds.reshape(-1).astype(jnp.int32)


def shard_levels(rng, dims, pieces, low, largest):
    gain, own = 1.0, jax.random.fold_in(rng, 6)
    for position, parts in pieces:
        steps = jnp.exp(jax.random.uniform(jax.random.fold_in(own, position), (parts,), jnp.float32, low / len(pieces), largest / len(pieces)))
        gain = gain * jnp.repeat(steps, dims[position] // parts).reshape([-1 if axis == position else 1 for axis in range(len(dims))])
    return gain


def normal_values(rng, extent, deviation, most, shards=(), kind=jnp.bfloat16):
    entries = deviation * jax.random.normal(rng, extent, jnp.float32)
    if shards:
        entries = entries * shard_levels(rng, extent, shards, -0.22, 0.18)
    return jnp.clip(entries, -most, most).astype(kind)


def setup_inputs(seed: int = 0) -> dict:
    streams_of = jax.random.split(jax.random.key(seed), 6)
    return {
        "design": normal_values(streams_of[0], (ROWS, P_SIZE), ROWS ** -0.5, 0.0625, ((0, 4), (1, 32))),
        "weights": jnp.clip(jnp.exp(math.log(5.0) - 3.218876 * jax.random.uniform(streams_of[1], (ROWS,), jnp.float32) ** shard_levels(streams_of[1], (ROWS,), ((0, 4),), -0.2, 0.2)), 0.2, 5.0),
        "response": normal_values(streams_of[2], (ROWS,), 1.0, 6.0, ((0, 4),), jnp.float32),
        "fold_of": draw_fold_of(jax.random.fold_in(streams_of[5], 71), 0),
        "smoothing": jnp.clip(jnp.exp(math.log(1.0) - 2.9957323 * jax.random.uniform(streams_of[4], (TERMS,), jnp.float32) ** shard_levels(streams_of[4], (TERMS,), ((0, 32),), -0.2, 0.2)), 0.05, 1.0),
    }


def second_differences(width):
    rows = lax.broadcasted_iota(jnp.int32, (width - 2, width), 0)
    cols = lax.broadcasted_iota(jnp.int32, (width - 2, width), 1)
    diffs = jnp.where(cols == rows, 1.0, 0.0) + jnp.where(cols == rows + 1, -2.0, 0.0) + jnp.where(cols == rows + 2, 1.0, 0.0)
    diffs = diffs.astype(jnp.float32)
    return jnp.dot(diffs.T, diffs, precision=lax.Precision.HIGHEST, preferred_element_type=jnp.float32)

def reference(design, weights, response, fold_of, smoothing):
    root_w = jnp.sqrt(weights)
    rooted = (design.astype(jnp.float32) * root_w[:, None]).astype(jnp.bfloat16)
    target = root_w * response
    slabs = rooted.reshape(-1, SLAB, P_SIZE)
    target_slabs = target.reshape(-1, SLAB)

    def add_slab(carry, item):
        grams, rhs = carry
        block, tvec, fid = item
        gram = jnp.dot(block.T, block, preferred_element_type=jnp.float32)
        right = jnp.dot(tvec, block.astype(jnp.float32), precision=lax.Precision.HIGHEST, preferred_element_type=jnp.float32)
        return ((grams.at[fid].add(gram), rhs.at[fid].add(right)), None)
    start = (jnp.zeros((FOLDS, P_SIZE, P_SIZE), jnp.float32), jnp.zeros((FOLDS, P_SIZE), jnp.float32))
    (grams, rhs), _ = lax.scan(add_slab, start, (slabs, target_slabs, fold_of.astype(jnp.int32)))
    total = lax.optimization_barrier(jnp.sum(grams, axis=0))
    total_rhs = lax.optimization_barrier(jnp.sum(rhs, axis=0))
    penalty = jnp.kron(jnp.diag(smoothing), second_differences(TERM))
    complement = total[None] - grams + penalty[None]
    return (complement, total_rhs[None] - rhs)
```

```python
import jax
import jax.numpy as jnp
from jax import lax
from jax.experimental import pallas as pl
from jax.experimental.pallas import tpu as pltpu
from jax.sharding import PartitionSpec as P


TERM = 64
AXES = ("fold", "tile")


def second_differences(width):
    rows = lax.broadcasted_iota(jnp.int32, (width - 2, width), 0)
    cols = lax.broadcasted_iota(jnp.int32, (width - 2, width), 1)
    diffs = (
        jnp.where(cols == rows, 1.0, 0.0)
        + jnp.where(cols == rows + 1, -2.0, 0.0)
        + jnp.where(cols == rows + 2, 1.0, 0.0)
    )
    diffs = diffs.astype(jnp.float32)
    return jnp.dot(
        diffs.T, diffs, precision=lax.Precision.HIGHEST, preferred_element_type=jnp.float32
    )


def flat(h, c, y, l, z):
    return (h * 2 + c) * 32 + y * 8 + l * 4 + z


def perm(move):
    pairs = []
    for h in range(2):
        for c in range(2):
            for y in range(4):
                for l in range(2):
                    for z in range(4):
                        pairs.append((flat(h, c, y, l, z), flat(*move(h, c, y, l, z))))
    return pairs


STEP = {
    ("y", 1): perm(lambda h, c, y, l, z: (h, c, (y + 1) % 4, l, z)),
    ("y", -1): perm(lambda h, c, y, l, z: (h, c, (y - 1) % 4, l, z)),
    ("z", 1): perm(lambda h, c, y, l, z: (h, c, y, l, (z + 1) % 4)),
    ("z", -1): perm(lambda h, c, y, l, z: (h, c, y, l, (z - 1) % 4)),
}
TURN = {
    ("y", 1): perm(lambda h, c, y, l, z: (h, c, (y + 1 - 2 * c) % 4, l, z)),
    ("y", -1): perm(lambda h, c, y, l, z: (h, c, (y - 1 + 2 * c) % 4, l, z)),
    ("z", 1): perm(lambda h, c, y, l, z: (h, c, y, l, (z + 1 - 2 * c) % 4)),
    ("z", -1): perm(lambda h, c, y, l, z: (h, c, y, l, (z - 1 + 2 * c) % 4)),
}
PARTNER = perm(lambda h, c, y, l, z: (h, c, y, 1 - l, z))
CORE = perm(lambda h, c, y, l, z: (h, 1 - c, y, l, z))
ACROSS = perm(lambda h, c, y, l, z: (1 - h, c, y, l if c == 0 else 1 - l, z))
OTHER = perm(lambda h, c, y, l, z: (1 - h, c, y, l, z))
MIB = 1 << 20
VMEM = 48 * MIB


def gram_kernel(slabs, local, r0, r1, *refs):
    xs, (g_ref, s_ref) = refs[:-2], refs[-2:]
    i = pl.program_id(0)
    size = r0.shape[1] // slabs
    g_ref[...] = jnp.zeros_like(g_ref)
    for k, x in enumerate(xs):

        @pl.when(i == k)
        def _(k=k, x=x):
            for t in range(slabs):
                part = pl.ds(t * size, size)
                for r, left in enumerate((r0, r1)[: 2 if k < 4 else 1]):
                    g_ref[2 * r + local[t]] += lax.dot_general(
                        left[:, part],
                        x[:, part],
                        (((1,), (1,)), ((), ())),
                        preferred_element_type=jnp.float32,
                    )

    for r in range(2):
        s_ref[r] = g_ref[2 * r] + g_ref[2 * r + 1]


def gram(local, rooted, partner, xs):
    rows, m = rooted.shape[1], len(xs)
    whole = pl.BlockSpec((256, rows), lambda i, f: (0, 0))
    return pl.pallas_call(
        lambda *refs: gram_kernel(local.shape[0], *refs),
        grid_spec=pltpu.PrefetchScalarGridSpec(
            num_scalar_prefetch=1,
            grid=(m,),
            in_specs=[whole] * (m + 2),
            out_specs=[
                pl.BlockSpec((4, 256, 256), lambda i, f: (0, 0, i)),
                pl.BlockSpec((2, 256, 256), lambda i, f: (0, 0, i)),
            ],
        ),
        out_shape=[
            pltpu.HBM((4, 256, 256 * m), jnp.float32),
            pltpu.HBM((2, 256, 256 * m), jnp.float32),
        ],
        compiler_params=pltpu.CompilerParams(vmem_limit_bytes=VMEM),
        cost_estimate=pl.CostEstimate(
            flops=2 * 512 * 256 * m * rows, bytes_accessed=4 * m * MIB, transcendentals=0
        ),
    )(local, rooted, partner, *xs)


def mix_kernel(r_ref, g1, s1, sr, tr, *refs):
    d_ref, u_ref = refs[-2:]
    other = s1[0]
    d_ref[0] = (g1[1] + other).astype(jnp.bfloat16)
    d_ref[1] = (g1[0] + other).astype(jnp.bfloat16)
    u_ref[...] = (sr[0] + tr[0]).astype(jnp.bfloat16)


def mix(pick, g, s, swapped, skip, u):
    extra = [] if u is None else [u]
    base = 4 * len(extra)
    width = 1024 - 256 * skip
    return pl.pallas_call(
        mix_kernel,
        grid_spec=pltpu.PrefetchScalarGridSpec(
            num_scalar_prefetch=1,
            grid=(4,),
            in_specs=[
                pl.BlockSpec((2, 256, 256), lambda i, r: (1, 0, i)),
                pl.BlockSpec((1, 256, 256), lambda i, r: (1, 0, i)),
                pl.BlockSpec((1, 256, 256), lambda i, r: (r[0], 0, i)),
                pl.BlockSpec((1, 256, 256), lambda i, r: (r[0], 0, i)),
            ]
            + [pl.BlockSpec(memory_space=pl.ANY)] * len(extra),
            out_specs=[
                pl.BlockSpec((2, 256, 256), lambda i, r: (0, 0, jnp.maximum(i - skip, 0))),
                pl.BlockSpec((256, 256), lambda i, r: (0, i + base)),
            ],
        ),
        out_shape=[
            pltpu.HBM((2, 256, width), jnp.bfloat16),
            pltpu.HBM((256, 2048), jnp.bfloat16),
        ],
        input_output_aliases={5: 1} if extra else {},
        compiler_params=pltpu.CompilerParams(vmem_limit_bytes=VMEM),
        cost_estimate=pl.CostEstimate(flops=MIB, bytes_accessed=8 * MIB, transcendentals=0),
    )(pick, g, swapped, s, swapped, *extra)


def final_kernel(first, pick, cols, g0, s0, mine, theirs, dr, *refs):
    out, buf, sems = refs[-3:]
    n = pl.program_id(0)
    slot = lax.rem(n, 2)
    swap = pick[0] == 0

    def copies(step, slot):
        return [
            pltpu.make_async_copy(
                buf.at[slot, j, :, :, pl.ds(128 * k, 128)],
                out.at[:, :, pl.ds(pl.multiple_of(cols[4 * step + 2 * k + j] * 128, 128), 128)],
                sems.at[slot, j, k],
            )
            for j in range(2)
            for k in range(2)
        ]

    @pl.when(n >= 2)
    def _():
        for copy in copies(n - 2, slot):
            copy.wait()

    a, b = mine[...].astype(jnp.float32), theirs[...].astype(jnp.float32)
    rest = s0[0] + jnp.where(swap, a, b)
    if first:
        rest = rest + jnp.where(n == 0, refs[0][...], 0.0)
    buf[slot, 0, 0] = g0[1] + rest
    buf[slot, 0, 1] = g0[0] + rest
    rest = jnp.where(swap, b, a)
    if first:

        @pl.when(n == 0)
        def _():
            gp, sp = refs[1], refs[2]
            buf[slot, 1, 0] = gp[1] + sp[0] + rest
            buf[slot, 1, 1] = gp[0] + sp[0] + rest

    @pl.when(n >= (1 if first else 0))
    def _():
        buf[slot, 1, 0] = dr[0].astype(jnp.float32) + rest
        buf[slot, 1, 1] = dr[1].astype(jnp.float32) + rest

    for copy in copies(n, slot):
        copy.start()

    @pl.when(n == 3)
    def _():
        for step in (2, 3):
            for copy in copies(step, step % 2):
                copy.wait()


def final(pick, cols, g, swapped, mine, theirs, half, dr, pen, out, total):
    first = out is None
    skip = 1 if first else 0
    base = 4 * half
    if first:
        extra = [pen, g, swapped]
        extra_specs = [
            pl.BlockSpec((256, 256), lambda n, p, c: (0, 0)),
            pl.BlockSpec((2, 256, 256), lambda n, p, c: (0, 0, 4)),
            pl.BlockSpec((1, 256, 256), lambda n, p, c: (0, 0, 4)),
        ]
    else:
        extra, extra_specs = [out], [pl.BlockSpec(memory_space=pl.ANY)]
    return pl.pallas_call(
        lambda *refs: final_kernel(first, *refs),
        grid_spec=pltpu.PrefetchScalarGridSpec(
            num_scalar_prefetch=2,
            grid=(4,),
            in_specs=[
                pl.BlockSpec((2, 256, 256), lambda n, p, c: (0, 0, n)),
                pl.BlockSpec((1, 256, 256), lambda n, p, c: (0, 0, n)),
                pl.BlockSpec((256, 256), lambda n, p, c: (0, n + base)),
                pl.BlockSpec((256, 256), lambda n, p, c: (0, n + base)),
                pl.BlockSpec((2, 256, 256), lambda n, p, c: (0, 0, jnp.maximum(n - skip, 0))),
            ]
            + extra_specs,
            out_specs=pl.BlockSpec(memory_space=pl.ANY),
            scratch_shapes=[
                pltpu.VMEM((2, 2, 2, 256, 256), jnp.float32),
                pltpu.SemaphoreType.DMA((2, 2, 2)),
            ],
        ),
        out_shape=pltpu.HBM((2, 256, total), jnp.float32),
        input_output_aliases={} if first else {7: 0},
        compiler_params=pltpu.CompilerParams(vmem_limit_bytes=VMEM),
        cost_estimate=pl.CostEstimate(flops=MIB, bytes_accessed=9 * MIB, transcendentals=0),
    )(pick, cols, g, swapped, mine, theirs, dr, *extra)


def body(design, weights, response, fold_of, smoothing):
    rows, block = design.shape
    slabs = fold_of.shape[0]
    width = block * 32
    fold, tile = lax.axis_index("fold"), lax.axis_index("tile")
    core = lax.rem(fold, 2)
    me_y, me_l, me_z = tile // 8, lax.rem(tile // 4, 2), lax.rem(tile, 4)
    pick = core.reshape(1).astype(jnp.int32)
    local = fold_of - 2 * fold

    def send(x, pairs):
        return lax.ppermute(x, AXES, pairs)

    root_w = jnp.sqrt(weights)
    rooted = (design.astype(jnp.float32) * root_w[:, None]).astype(jnp.bfloat16).T
    rooted = lax.optimization_barrier(rooted)
    partner = send(rooted, PARTNER)

    target = root_w * response
    member = jnp.repeat(local, rows // slabs)
    prod = rooted.astype(jnp.float32) * target[None, :]
    rhs = jnp.stack([jnp.sum(jnp.where(member == f, prod, 0.0), axis=1) for f in range(2)])
    chip_rhs = jnp.sum(rhs, axis=0)
    chip_rhs = chip_rhs + send(chip_rhs, CORE)
    total_rhs = chip_rhs + send(chip_rhs, OTHER)
    complement_rhs = total_rhs[None] - rhs

    near, chunks = [], ([], [], [])
    where = ([], [], [], [])
    where[0].extend([(0, 0, 0), (0, 0, 1)])
    far = []
    for colour, (p, q) in enumerate((("y", "z"), ("z", "y"))):
        at = lambda u, v, p=p, k=colour: (u, v, k) if p == "y" else (v, u, k)
        own = rooted[128 * colour : 128 * (colour + 1)]
        a = send(own, TURN[p, 1])
        b = send(own, TURN[p, -1])
        d = send(a, TURN[p, 1])
        ab = jnp.concatenate([jnp.where(core == 0, a, b), jnp.where(core == 0, b, a)], axis=0)
        ab_m, ab_p = send(ab, STEP[q, 1]), send(ab, STEP[q, -1])
        od = jnp.concatenate([own, d], axis=0)
        od_m, od_p = send(od, STEP[q, 1]), send(od, STEP[q, -1])
        ab_2 = send(ab_m, STEP[q, 1])
        od_2 = send(od_p, STEP[q, -1])
        near.append(ab)
        far.append(d)
        chunks[0].extend([ab_m, ab_p])
        chunks[1].extend([od_m, od_p])
        chunks[2].extend([ab_2, od_2])
        ab_off, od_off = (-1, 1), (0, 2)
        where[0].extend(at(o, 0) for o in ab_off)
        where[1].extend(at(o, v) for v in (-1, 1) for o in ab_off)
        where[2].extend(at(o, v) for v in (-1, 1) for o in od_off)
        where[3].extend(at(o, 2) for o in ab_off + od_off)
    where[0].extend([(2, 0, 0), (0, 2, 1)])
    work = [[rooted] + near + [jnp.concatenate(far, axis=0), partner]] + list(chunks)

    pen = jnp.kron(jnp.diag(smoothing), second_differences(TERM))

    state, mine, theirs, u = [], [], [], None
    for n, xs in enumerate(work):
        g, s = gram(local, rooted, partner, xs)
        swapped = send(s, CORE)
        give, u = mix(pick, g, s, swapped, 1 if n == 0 else 0, u)
        dr = send(give, PARTNER)
        state.append((g, swapped, dr))
        if n % 2 == 1:
            mine.append(send(u, ACROSS))
            theirs.append(send(mine[-1], CORE))
            u = None
    out = None
    for n, (g, swapped, dr) in enumerate(state):
        cols = []
        for dy, dz, colour in where[n]:
            y, z = lax.rem(me_y + dy + 4, 4), lax.rem(me_z + dz + 4, 4)
            for l in (me_l, 1 - me_l):
                cols.append((y * 8 + l * 4 + z) * 2 + colour)
        cols = jnp.stack(cols).astype(jnp.int32)
        out = final(
            pick, cols, g, swapped, mine[n // 2], theirs[n // 2], n % 2, dr, pen, out, width
        )
    return (out, complement_rhs)


def solution(mesh):
    in_specs = (P("fold", "tile"), P("fold"), P("fold"), P("fold"), P("tile"))
    out_specs = (P("fold", "tile", None), P("fold", "tile"))

    return jax.shard_map(body, mesh=mesh, in_specs=in_specs, out_specs=out_specs, check_vma=False)
```

```python
import jax
import jax.numpy as jnp
from jax import lax
from jax.experimental import pallas as pl
from jax.experimental.pallas import tpu as pltpu
from jax.sharding import PartitionSpec as P


TERM = 64
AXES = ("fold", "tile")


def second_differences(width):
    rows = lax.broadcasted_iota(jnp.int32, (width - 2, width), 0)
    cols = lax.broadcasted_iota(jnp.int32, (width - 2, width), 1)
    diffs = (
        jnp.where(cols == rows, 1.0, 0.0)
        + jnp.where(cols == rows + 1, -2.0, 0.0)
        + jnp.where(cols == rows + 2, 1.0, 0.0)
    )
    diffs = diffs.astype(jnp.float32)
    return jnp.dot(
        diffs.T, diffs, precision=lax.Precision.HIGHEST, preferred_element_type=jnp.float32
    )


def flat(h, c, y, l, z):
    return (h * 2 + c) * 32 + y * 8 + l * 4 + z


def perm(move):
    pairs = []
    for h in range(2):
        for c in range(2):
            for y in range(4):
                for l in range(2):
                    for z in range(4):
                        pairs.append((flat(h, c, y, l, z), flat(*move(h, c, y, l, z))))
    return pairs


STEP = {
    ("y", 1): perm(lambda h, c, y, l, z: (h, c, (y + 1) % 4, l, z)),
    ("y", -1): perm(lambda h, c, y, l, z: (h, c, (y - 1) % 4, l, z)),
    ("z", 1): perm(lambda h, c, y, l, z: (h, c, y, l, (z + 1) % 4)),
    ("z", -1): perm(lambda h, c, y, l, z: (h, c, y, l, (z - 1) % 4)),
}
TURN = {
    ("y", 1): perm(lambda h, c, y, l, z: (h, c, (y + 1 - 2 * c) % 4, l, z)),
    ("y", -1): perm(lambda h, c, y, l, z: (h, c, (y - 1 + 2 * c) % 4, l, z)),
    ("z", 1): perm(lambda h, c, y, l, z: (h, c, y, l, (z + 1 - 2 * c) % 4)),
    ("z", -1): perm(lambda h, c, y, l, z: (h, c, y, l, (z - 1 + 2 * c) % 4)),
}
PARTNER = perm(lambda h, c, y, l, z: (h, c, y, 1 - l, z))
CORE = perm(lambda h, c, y, l, z: (h, 1 - c, y, l, z))
ACROSS = perm(lambda h, c, y, l, z: (1 - h, c, y, l if c == 0 else 1 - l, z))
OTHER = perm(lambda h, c, y, l, z: (1 - h, c, y, l, z))
MIB = 1 << 20
VMEM = 48 * MIB


def gram_kernel(slabs, local, r0, r1, *refs):
    xs, (own_ref, give_ref, sum_ref, acc) = refs[:-4], refs[-4:]
    i = pl.program_id(0)
    size = r0.shape[1] // slabs
    own_ref[...] = jnp.zeros_like(own_ref)
    acc[...] = jnp.zeros_like(acc)
    for k, x in enumerate(xs):

        @pl.when(i == k)
        def _(k=k, x=x):
            for t in range(slabs):
                part = pl.ds(t * size, size)
                for left, to in ((r0, own_ref), (r1, acc))[: 2 if k < 4 else 1]:
                    to[local[t]] += lax.dot_general(
                        left[:, part],
                        x[:, part],
                        (((1,), (1,)), ((), ())),
                        preferred_element_type=jnp.float32,
                    )

    sum_ref[0] = own_ref[0] + own_ref[1]
    sum_ref[1] = acc[0] + acc[1]

    @pl.when(i < 4)
    def _():
        give_ref[...] = acc[...].astype(jnp.bfloat16)


def gram(local, rooted, partner, xs, skip):
    rows, m = rooted.shape[1], len(xs)
    whole = pl.BlockSpec((256, rows), lambda i, f: (0, 0))
    last = 3 - skip
    return pl.pallas_call(
        lambda *refs: gram_kernel(local.shape[0], *refs),
        grid_spec=pltpu.PrefetchScalarGridSpec(
            num_scalar_prefetch=1,
            grid=(m,),
            in_specs=[whole] * (m + 2),
            out_specs=[
                pl.BlockSpec((2, 256, 256), lambda i, f: (0, 0, i)),
                pl.BlockSpec((2, 256, 256), lambda i, f: (0, 0, jnp.clip(i - skip, 0, last))),
                pl.BlockSpec((2, 256, 256), lambda i, f: (0, 0, i)),
            ],
            scratch_shapes=[pltpu.VMEM((2, 256, 256), jnp.float32)],
        ),
        out_shape=[
            pltpu.HBM((2, 256, 256 * m), jnp.float32),
            pltpu.HBM((2, 256, 256 * (last + 1)), jnp.bfloat16),
            pltpu.HBM((2, 256, 256 * m), jnp.float32),
        ],
        compiler_params=pltpu.CompilerParams(vmem_limit_bytes=VMEM),
        cost_estimate=pl.CostEstimate(
            flops=2 * 512 * 256 * m * rows, bytes_accessed=3 * m * MIB, transcendentals=0
        ),
    )(local, rooted, partner, *xs)


def mix_kernel(r_ref, mine, theirs, *refs):
    refs[-1][...] = (mine[0] + theirs[0]).astype(jnp.bfloat16)


def mix(pick, s, swapped, half, parts, u):
    extra = [] if u is None else [u]
    base = 2 * half
    return pl.pallas_call(
        mix_kernel,
        grid_spec=pltpu.PrefetchScalarGridSpec(
            num_scalar_prefetch=1,
            grid=(2,),
            in_specs=[
                pl.BlockSpec((1, 256, 512), lambda i, r: (r[0], 0, i)),
                pl.BlockSpec((1, 256, 512), lambda i, r: (r[0], 0, i)),
            ]
            + [pl.BlockSpec(memory_space=pl.ANY)] * len(extra),
            out_specs=pl.BlockSpec((256, 512), lambda i, r: (0, i + base)),
        ),
        out_shape=pltpu.HBM((256, 1024 * parts), jnp.bfloat16),
        input_output_aliases={3: 0} if extra else {},
        compiler_params=pltpu.CompilerParams(vmem_limit_bytes=VMEM),
        cost_estimate=pl.CostEstimate(flops=MIB, bytes_accessed=3 * MIB, transcendentals=0),
    )(pick, s, swapped, *extra)


def final_kernel(first, pick, cols, g0, s0, mine, theirs, dr, er, *refs):
    out, buf, sems = refs[-3:]
    n = pl.program_id(0)
    slot = lax.rem(n, 2)
    swap = pick[0] == 0

    def copies(step, slot):
        return [
            pltpu.make_async_copy(
                buf.at[slot, j, :, :, pl.ds(128 * k, 128)],
                out.at[:, :, pl.ds(pl.multiple_of(cols[4 * step + 2 * k + j] * 128, 128), 128)],
                sems.at[slot, j, k],
            )
            for j in range(2)
            for k in range(2)
        ]

    @pl.when(n >= 2)
    def _():
        for copy in copies(n - 2, slot):
            copy.wait()

    a, b = mine[...].astype(jnp.float32), theirs[...].astype(jnp.float32)
    rest = s0[0] + jnp.where(swap, a, b)
    if first:
        rest = rest + jnp.where(n == 0, refs[0][...], 0.0)
    buf[slot, 0, 0] = g0[1] + rest
    buf[slot, 0, 1] = g0[0] + rest
    rest = jnp.where(swap, b, a)
    if first:

        @pl.when(n == 0)
        def _():
            gp, sp = refs[1], refs[2]
            buf[slot, 1, 0] = gp[1] + sp[0] + rest
            buf[slot, 1, 1] = gp[0] + sp[0] + rest

    @pl.when(n >= (1 if first else 0))
    def _():
        other = er[0].astype(jnp.float32) + er[1].astype(jnp.float32) + rest
        buf[slot, 1, 0] = dr[1].astype(jnp.float32) + other
        buf[slot, 1, 1] = dr[0].astype(jnp.float32) + other

    for copy in copies(n, slot):
        copy.start()

    @pl.when(n == 3)
    def _():
        for step in (2, 3):
            for copy in copies(step, step % 2):
                copy.wait()


def final(pick, cols, g, swapped, mine, theirs, half, dr, er, pen, out, total):
    first = out is None
    skip = 1 if first else 0
    base = 4 * half
    if first:
        extra = [pen, g, swapped]
        extra_specs = [
            pl.BlockSpec((256, 256), lambda n, p, c: (0, 0)),
            pl.BlockSpec((2, 256, 256), lambda n, p, c: (0, 0, 4)),
            pl.BlockSpec((1, 256, 256), lambda n, p, c: (0, 0, 4)),
        ]
    else:
        extra, extra_specs = [out], [pl.BlockSpec(memory_space=pl.ANY)]
    return pl.pallas_call(
        lambda *refs: final_kernel(first, *refs),
        grid_spec=pltpu.PrefetchScalarGridSpec(
            num_scalar_prefetch=2,
            grid=(4,),
            in_specs=[
                pl.BlockSpec((2, 256, 256), lambda n, p, c: (0, 0, n)),
                pl.BlockSpec((1, 256, 256), lambda n, p, c: (0, 0, n)),
                pl.BlockSpec((256, 256), lambda n, p, c: (0, n + base)),
                pl.BlockSpec((256, 256), lambda n, p, c: (0, n + base)),
            ]
            + [pl.BlockSpec((2, 256, 256), lambda n, p, c: (0, 0, jnp.maximum(n - skip, 0)))] * 2
            + extra_specs,
            out_specs=pl.BlockSpec(memory_space=pl.ANY),
            scratch_shapes=[
                pltpu.VMEM((2, 2, 2, 256, 256), jnp.float32),
                pltpu.SemaphoreType.DMA((2, 2, 2)),
            ],
        ),
        out_shape=pltpu.HBM((2, 256, total), jnp.float32),
        input_output_aliases={} if first else {8: 0},
        compiler_params=pltpu.CompilerParams(vmem_limit_bytes=VMEM),
        cost_estimate=pl.CostEstimate(flops=MIB, bytes_accessed=9 * MIB, transcendentals=0),
    )(pick, cols, g, swapped, mine, theirs, dr, er, *extra)


def body(design, weights, response, fold_of, smoothing):
    rows, block = design.shape
    slabs = fold_of.shape[0]
    width = block * 32
    fold, tile = lax.axis_index("fold"), lax.axis_index("tile")
    core = lax.rem(fold, 2)
    me_y, me_l, me_z = tile // 8, lax.rem(tile // 4, 2), lax.rem(tile, 4)
    pick = core.reshape(1).astype(jnp.int32)
    local = fold_of - 2 * fold

    def send(x, pairs):
        return lax.ppermute(x, AXES, pairs)

    root_w = jnp.sqrt(weights)
    rooted = (design.astype(jnp.float32) * root_w[:, None]).astype(jnp.bfloat16).T
    rooted = lax.optimization_barrier(rooted)
    partner = send(rooted, PARTNER)

    target = root_w * response
    member = jnp.repeat(local, rows // slabs)
    prod = rooted.astype(jnp.float32) * target[None, :]
    rhs = jnp.stack([jnp.sum(jnp.where(member == f, prod, 0.0), axis=1) for f in range(2)])
    chip_rhs = jnp.sum(rhs, axis=0)
    chip_rhs = chip_rhs + send(chip_rhs, CORE)
    total_rhs = chip_rhs + send(chip_rhs, OTHER)
    complement_rhs = total_rhs[None] - rhs

    near, chunks = [], ([], [], [])
    where = ([], [], [], [])
    where[0].extend([(0, 0, 0), (0, 0, 1)])
    far = []
    for colour, (p, q) in enumerate((("y", "z"), ("z", "y"))):
        at = lambda u, v, p=p, k=colour: (u, v, k) if p == "y" else (v, u, k)
        own = rooted[128 * colour : 128 * (colour + 1)]
        a = send(own, TURN[p, 1])
        b = send(own, TURN[p, -1])
        d = send(a, TURN[p, 1])
        ab = jnp.concatenate([jnp.where(core == 0, a, b), jnp.where(core == 0, b, a)], axis=0)
        ab_m, ab_p = send(ab, STEP[q, 1]), send(ab, STEP[q, -1])
        od = jnp.concatenate([own, d], axis=0)
        od_m, od_p = send(od, STEP[q, 1]), send(od, STEP[q, -1])
        ab_2 = send(ab_m, STEP[q, 1])
        od_2 = send(od_p, STEP[q, -1])
        near.append(ab)
        far.append(d)
        chunks[0].extend([ab_m, ab_p])
        chunks[1].extend([od_m, od_p])
        chunks[2].extend([ab_2, od_2])
        ab_off, od_off = (-1, 1), (0, 2)
        where[0].extend(at(o, 0) for o in ab_off)
        where[1].extend(at(o, v) for v in (-1, 1) for o in ab_off)
        where[2].extend(at(o, v) for v in (-1, 1) for o in od_off)
        where[3].extend(at(o, 2) for o in ab_off + od_off)
    where[0].extend([(2, 0, 0), (0, 2, 1)])
    work = [[rooted] + near + [jnp.concatenate(far, axis=0), partner]] + list(chunks)

    pen = jnp.kron(jnp.diag(smoothing), second_differences(TERM))

    places = ((0, 0, 2), (0, 1, 2), (1, 0, 1), (2, 0, 1))
    state, mine, theirs, u = [], [], [], None
    for n, xs in enumerate(work):
        message, half, parts = places[n]
        g, give, s = gram(local, rooted, partner, xs, 1 if n == 0 else 0)
        swapped = send(s, CORE)
        dr = send(give, PARTNER)
        er = send(dr, CORE)
        u = mix(pick, s, swapped, half, parts, u)
        state.append((g, swapped, dr, er))
        if half == parts - 1:
            mine.append(send(u, ACROSS))
            theirs.append(send(mine[-1], CORE))
            u = None
    out = None
    for n, (g, swapped, dr, er) in enumerate(state):
        message, half, _ = places[n]
        cols = []
        for dy, dz, colour in where[n]:
            y, z = lax.rem(me_y + dy + 4, 4), lax.rem(me_z + dz + 4, 4)
            for l in (me_l, 1 - me_l):
                cols.append((y * 8 + l * 4 + z) * 2 + colour)
        cols = jnp.stack(cols).astype(jnp.int32)
        out = final(
            pick, cols, g, swapped, mine[message], theirs[message], half, dr, er, pen, out, width
        )
    return (out, complement_rhs)


def solution(mesh):
    in_specs = (P("fold", "tile"), P("fold"), P("fold"), P("fold"), P("tile"))
    out_specs = (P("fold", "tile", None), P("fold", "tile"))

    return jax.shard_map(body, mesh=mesh, in_specs=in_specs, out_specs=out_specs, check_vma=False)
```

```python
import jax
import jax.numpy as jnp
from jax import lax
from jax.experimental import pallas as pl
from jax.experimental.pallas import tpu as pltpu
from jax.sharding import PartitionSpec as P


TERM = 64
AXES = ("fold", "tile")


def second_differences(width):
    rows = lax.broadcasted_iota(jnp.int32, (width - 2, width), 0)
    cols = lax.broadcasted_iota(jnp.int32, (width - 2, width), 1)
    diffs = (
        jnp.where(cols == rows, 1.0, 0.0)
        + jnp.where(cols == rows + 1, -2.0, 0.0)
        + jnp.where(cols == rows + 2, 1.0, 0.0)
    )
    diffs = diffs.astype(jnp.float32)
    return jnp.dot(
        diffs.T, diffs, precision=lax.Precision.HIGHEST, preferred_element_type=jnp.float32
    )


def flat(h, c, y, l, z):
    return (h * 2 + c) * 32 + y * 8 + l * 4 + z


def perm(move):
    pairs = []
    for h in range(2):
        for c in range(2):
            for y in range(4):
                for l in range(2):
                    for z in range(4):
                        pairs.append((flat(h, c, y, l, z), flat(*move(h, c, y, l, z))))
    return pairs


STEP = {
    ("y", 1): perm(lambda h, c, y, l, z: (h, c, (y + 1) % 4, l, z)),
    ("y", -1): perm(lambda h, c, y, l, z: (h, c, (y - 1) % 4, l, z)),
    ("z", 1): perm(lambda h, c, y, l, z: (h, c, y, l, (z + 1) % 4)),
    ("z", -1): perm(lambda h, c, y, l, z: (h, c, y, l, (z - 1) % 4)),
}
TURN = {
    ("y", 1): perm(lambda h, c, y, l, z: (h, c, (y + 1 - 2 * c) % 4, l, z)),
    ("y", -1): perm(lambda h, c, y, l, z: (h, c, (y - 1 + 2 * c) % 4, l, z)),
    ("z", 1): perm(lambda h, c, y, l, z: (h, c, y, l, (z + 1 - 2 * c) % 4)),
    ("z", -1): perm(lambda h, c, y, l, z: (h, c, y, l, (z - 1 + 2 * c) % 4)),
}
PARTNER = perm(lambda h, c, y, l, z: (h, c, y, 1 - l, z))
CORE = perm(lambda h, c, y, l, z: (h, 1 - c, y, l, z))
ACROSS = perm(lambda h, c, y, l, z: (1 - h, c, y, l if c == 0 else 1 - l, z))
OTHER = perm(lambda h, c, y, l, z: (1 - h, c, y, l, z))
MIB = 1 << 20


def gram_kernel(slabs, layout, skip, gives, count, local, r0, r1, *refs):
    xs, refs = refs[:count], refs[count:]
    own_ref, sum_ref = refs[0], refs[1]
    i = pl.program_id(0)
    size = r0.shape[1] // slabs
    own_ref[...] = jnp.zeros_like(own_ref)
    targets = [(r0, own_ref)]
    if gives:
        give_ref, acc = refs[2], refs[3]
        acc[...] = jnp.zeros_like(acc)
        targets.append((r1, acc))
    for k, ((a, ha), (b, hb)) in enumerate(layout):

        @pl.when(i == k)
        def _(k=k, a=xs[a], ha=ha, b=xs[b], hb=hb):
            for t in range(slabs):
                part = pl.ds(t * size, size)
                x = jnp.concatenate(
                    [a[pl.ds(128 * ha, 128), part], b[pl.ds(128 * hb, 128), part]], axis=0
                )
                for left, to in targets if k < 4 else targets[:1]:
                    to[local[t]] += lax.dot_general(
                        left[:, part],
                        x,
                        (((1,), (1,)), ((), ())),
                        preferred_element_type=jnp.float32,
                    )

    sum_ref[0] = own_ref[0] + own_ref[1]
    if gives:
        sum_ref[1] = acc[0] + acc[1]

        @pl.when((i >= skip) & (i < 4))
        def _():
            give_ref[...] = acc[...].astype(jnp.bfloat16)


def gram(local, rooted, partner, xs, layout, skip, gives):
    rows, m = rooted.shape[1], len(layout)
    whole = lambda x: pl.BlockSpec(
        x.shape, lambda i, f: (0, 0), pipeline_mode=pl.Buffered(1)
    )
    last = 3 - skip
    rank = 2 if gives else 1
    out_specs = [
        pl.BlockSpec((2, 256, 256), lambda i, f: (0, 0, i)),
        pl.BlockSpec((rank, 256, 256), lambda i, f: (0, 0, i)),
    ]
    out_shape = [
        pltpu.HBM((2, 256, 256 * m), jnp.float32),
        pltpu.HBM((rank, 256, 256 * m), jnp.float32),
    ]
    if gives:
        out_specs.append(
            pl.BlockSpec((2, 256, 256), lambda i, f: (0, 0, jnp.clip(i - skip, 0, last)))
        )
        out_shape.append(pltpu.HBM((2, 256, 256 * (last + 1)), jnp.bfloat16))
    return pl.pallas_call(
        lambda *refs: gram_kernel(local.shape[0], layout, skip, gives, len(xs), *refs),
        grid_spec=pltpu.PrefetchScalarGridSpec(
            num_scalar_prefetch=1,
            grid=(m,),
            in_specs=[whole(x) for x in (rooted, partner, *xs)],
            out_specs=out_specs,
            scratch_shapes=[pltpu.VMEM((2, 256, 256), jnp.float32)] if gives else [],
        ),
        out_shape=out_shape,
        compiler_params=pltpu.CompilerParams(vmem_limit_bytes=20 * MIB),
        cost_estimate=pl.CostEstimate(
            flops=2 * 512 * 256 * m * rows, bytes_accessed=3 * m * MIB, transcendentals=0
        ),
    )(local, rooted, partner, *xs)


def stay(x):
    return pltpu.with_memory_space_constraint(x, pltpu.HBM)


def mix_kernel(r_ref, mine, theirs, *refs):
    refs[-1][...] = (mine[0] + theirs[0]).astype(jnp.bfloat16)


def mix(pick, s, swapped, half, parts, u):
    extra = [] if u is None else [u]
    base = 2 * half
    return pl.pallas_call(
        mix_kernel,
        grid_spec=pltpu.PrefetchScalarGridSpec(
            num_scalar_prefetch=1,
            grid=(2,),
            in_specs=[
                pl.BlockSpec((1, 256, 512), lambda i, r: (r[0], 0, i)),
                pl.BlockSpec((1, 256, 512), lambda i, r: (r[0], 0, i)),
            ]
            + [pl.BlockSpec(memory_space=pl.ANY)] * len(extra),
            out_specs=pl.BlockSpec((256, 512), lambda i, r: (0, i + base)),
        ),
        out_shape=pltpu.HBM((256, 1024 * parts), jnp.bfloat16),
        input_output_aliases={3: 0} if extra else {},
        compiler_params=pltpu.CompilerParams(vmem_limit_bytes=8 * MIB),
        cost_estimate=pl.CostEstimate(flops=MIB, bytes_accessed=3 * MIB, transcendentals=0),
    )(pick, stay(s), swapped, *extra)


def final_kernel(diagonal, skip, pick, cols, g0, s0, mine, theirs, dr, er, *refs):
    out, buf, sems = refs[-3:]
    n = pl.program_id(0)
    slot = lax.rem(n, 2)
    swap = pick[0] == 0

    def copies(step, slot):
        return [
            pltpu.make_async_copy(
                buf.at[slot, j, :, :, pl.ds(128 * k, 128)],
                out.at[:, :, pl.ds(pl.multiple_of(cols[4 * step + 2 * k + j] * 128, 128), 128)],
                sems.at[slot, j, k],
            )
            for j in range(2)
            for k in range(2)
        ]

    @pl.when(n >= 2)
    def _():
        for copy in copies(n - 2, slot):
            copy.wait()

    a, b = mine[...].astype(jnp.float32), theirs[...].astype(jnp.float32)
    rest = s0[0] + jnp.where(swap, a, b)
    if diagonal:
        rest = rest + jnp.where(n == 0, refs[2][...], 0.0)
    buf[slot, 0, 0] = g0[1] + rest
    buf[slot, 0, 1] = g0[0] + rest
    rest = jnp.where(swap, b, a)
    if skip:

        @pl.when(n < skip)
        def _():
            gp, sp = refs[0], refs[1]
            buf[slot, 1, 0] = gp[1] + sp[0] + rest
            buf[slot, 1, 1] = gp[0] + sp[0] + rest

    @pl.when(n >= skip)
    def _():
        other = er[0].astype(jnp.float32) + er[1].astype(jnp.float32) + rest
        buf[slot, 1, 0] = dr[1].astype(jnp.float32) + other
        buf[slot, 1, 1] = dr[0].astype(jnp.float32) + other

    for copy in copies(n, slot):
        copy.start()

    @pl.when(n == 3)
    def _():
        for step in (2, 3):
            for copy in copies(step, step % 2):
                copy.wait()


def final(pick, cols, g, swapped, mine, theirs, half, dr, er, skip, known, pen, out, total):
    base = 4 * half
    extra, extra_specs, alias = [], [], {}
    if skip:
        gp, sp, at = known
        extra += [stay(gp), sp]
        extra_specs += [
            pl.BlockSpec((2, 256, 256), lambda n, p, c: (0, 0, at + jnp.minimum(n, skip - 1))),
            pl.BlockSpec((1, 256, 256), lambda n, p, c: (0, 0, at + jnp.minimum(n, skip - 1))),
        ]
    if out is None:
        extra.append(pen)
        extra_specs.append(pl.BlockSpec((256, 256), lambda n, p, c: (0, 0)))
    else:
        alias = {8 + len(extra): 0}
        extra.append(out)
        extra_specs.append(pl.BlockSpec(memory_space=pl.ANY))
    return pl.pallas_call(
        lambda *refs: final_kernel(out is None, skip, *refs),
        grid_spec=pltpu.PrefetchScalarGridSpec(
            num_scalar_prefetch=2,
            grid=(4,),
            in_specs=[
                pl.BlockSpec((2, 256, 256), lambda n, p, c: (0, 0, n)),
                pl.BlockSpec((1, 256, 256), lambda n, p, c: (0, 0, n)),
                pl.BlockSpec((256, 256), lambda n, p, c: (0, n + base)),
                pl.BlockSpec((256, 256), lambda n, p, c: (0, n + base)),
            ]
            + [pl.BlockSpec((2, 256, 256), lambda n, p, c: (0, 0, jnp.maximum(n - skip, 0)))] * 2
            + extra_specs,
            out_specs=pl.BlockSpec(memory_space=pl.ANY),
            scratch_shapes=[
                pltpu.VMEM((2, 2, 2, 256, 256), jnp.float32),
                pltpu.SemaphoreType.DMA((2, 2, 2)),
            ],
        ),
        out_shape=pltpu.HBM((2, 256, total), jnp.float32),
        input_output_aliases=alias,
        compiler_params=pltpu.CompilerParams(vmem_limit_bytes=12 * MIB),
        cost_estimate=pl.CostEstimate(flops=MIB, bytes_accessed=9 * MIB, transcendentals=0),
    )(pick, cols, stay(g), swapped, mine, theirs, dr, er, *extra)


def body(design, weights, response, fold_of, smoothing):
    rows, block = design.shape
    slabs = fold_of.shape[0]
    width = block * 32
    fold, tile = lax.axis_index("fold"), lax.axis_index("tile")
    core = lax.rem(fold, 2)
    me_y, me_l, me_z = tile // 8, lax.rem(tile // 4, 2), lax.rem(tile, 4)
    pick = core.reshape(1).astype(jnp.int32)
    local = fold_of - 2 * fold

    def send(x, pairs):
        return lax.ppermute(x, AXES, pairs)

    root_w = jnp.sqrt(weights)
    rooted = (design.astype(jnp.float32) * root_w[:, None]).astype(jnp.bfloat16).T
    rooted = lax.optimization_barrier(rooted)
    partner = send(rooted, PARTNER)

    target = root_w * response
    member = jnp.repeat(local, rows // slabs)
    prod = rooted.astype(jnp.float32) * target[None, :]
    rhs = jnp.stack([jnp.sum(jnp.where(member == f, prod, 0.0), axis=1) for f in range(2)])
    chip_rhs = jnp.sum(rhs, axis=0)
    chip_rhs = chip_rhs + send(chip_rhs, CORE)
    total_rhs = chip_rhs + send(chip_rhs, OTHER)
    complement_rhs = total_rhs[None] - rhs

    blocks = ([rooted], [], [], [])
    where = ([(0, 0, 0), (0, 0, 1)], [], [], [])
    far = []
    for colour, (p, q) in enumerate((("y", "z"), ("z", "y"))):
        at = lambda u, v, p=p, k=colour: (u, v, k) if p == "y" else (v, u, k)
        own = rooted[128 * colour : 128 * (colour + 1)]
        a = send(own, TURN[p, 1])
        b = send(own, TURN[p, -1])
        d = send(a, TURN[p, 1])
        ab = jnp.concatenate([jnp.where(core == 0, a, b), jnp.where(core == 0, b, a)], axis=0)
        ab_m, ab_p = send(ab, STEP[q, 1]), send(ab, STEP[q, -1])
        od = jnp.concatenate([own, d], axis=0)
        od_m, od_p = send(od, STEP[q, 1]), send(od, STEP[q, -1])
        ab_2 = send(ab_m, STEP[q, 1])
        od_2 = send(od_p, STEP[q, -1])
        blocks[0].append(ab)
        far.append(d)
        blocks[1].extend([ab_m, ab_p])
        blocks[2].extend([od_m, od_p])
        blocks[3].extend([ab_2, od_2])
        where[0].extend(at(o, 0) for o in (-1, 1))
        where[1].extend(at(o, v) for v in (-1, 1) for o in (-1, 1))
        where[2].extend(at(0, v) for v in (-1, 1))
        where[3].extend(at(o, 2) for o in (-1, 1, 0, 2))
    where[0].extend([(2, 0, 0), (0, 2, 1)])
    where[2].extend([(2, -1, 0), (2, 1, 0), (-1, 2, 1), (1, 2, 1)])
    blocks[0].extend(far + [partner])
    both = lambda k: ((k, 0), (k, 1))
    layouts = (
        (both(0), both(1), both(2), ((3, 0), (4, 0)), both(5)),
        tuple(both(k) for k in range(4)),
        tuple(((k, half), (k + 1, half)) for half in range(2) for k in (0, 2)),
        tuple(both(k) for k in range(4)),
    )
    skips = (1, 0, 2, 0)

    pen = jnp.kron(jnp.diag(smoothing), second_differences(TERM))
    halves = (partner[:128], partner[128:])
    local, pen, halves = lax.optimization_barrier((local, pen, halves))

    places = ((0, 0, 1), (1, 0, 1), (2, 0, 1), (3, 0, 1))
    state, mine, theirs, u = [], [], [], None
    for n, xs in enumerate(blocks):
        message, half, parts = places[n]
        g, s, give = gram(local, rooted, partner, xs, layouts[n], skips[n], True)
        swapped = send(s, CORE)
        dr = send(give, PARTNER)
        er = send(dr, CORE)
        u = mix(pick, s, swapped, half, parts, u)
        state.append((g, swapped, dr, er))
        if half == parts - 1:
            mine.append(send(u, ACROSS))
            theirs.append(send(mine[-1], CORE))
            u = None
    known = []
    for colour, q in enumerate("zy"):
        known.append(send(halves[colour], STEP[q, 1]))
        known.append(send(halves[colour], STEP[q, -1]))
    pair = lambda k: ((k, 0), (k + 1, 0))
    g_known, s = gram(local, rooted, partner, known, (pair(0), pair(2)), 0, False)
    s_known = send(s, CORE)
    raw = {0: (state[0][0], state[0][1], 4), 2: (g_known, s_known, 0)}
    out = None
    for n, (g, swapped, dr, er) in enumerate(state):
        message, half, _ = places[n]
        cols = []
        for dy, dz, colour in where[n]:
            y, z = lax.rem(me_y + dy + 4, 4), lax.rem(me_z + dz + 4, 4)
            for l in (me_l, 1 - me_l):
                cols.append((y * 8 + l * 4 + z) * 2 + colour)
        cols = jnp.stack(cols).astype(jnp.int32)
        v0, v1 = mine[message], theirs[message]
        out = final(
            pick, cols, g, swapped, v0, v1, half, dr, er, skips[n], raw.get(n), pen, out, width
        )
    return (out, complement_rhs)


def solution(mesh):
    in_specs = (P("fold", "tile"), P("fold"), P("fold"), P("fold"), P("tile"))
    out_specs = (P("fold", "tile", None), P("fold", "tile"))

    return jax.shard_map(body, mesh=mesh, in_specs=in_specs, out_specs=out_specs, check_vma=False)
```

```python
import jax
import jax.numpy as jnp
from jax import lax
from jax.experimental import pallas as pl
from jax.experimental.pallas import tpu as pltpu
from jax.sharding import PartitionSpec as P


TERM = 64
AXES = ("fold", "tile")


def second_differences(width):
    rows = lax.broadcasted_iota(jnp.int32, (width - 2, width), 0)
    cols = lax.broadcasted_iota(jnp.int32, (width - 2, width), 1)
    diffs = (
        jnp.where(cols == rows, 1.0, 0.0)
        + jnp.where(cols == rows + 1, -2.0, 0.0)
        + jnp.where(cols == rows + 2, 1.0, 0.0)
    )
    diffs = diffs.astype(jnp.float32)
    return jnp.dot(
        diffs.T, diffs, precision=lax.Precision.HIGHEST, preferred_element_type=jnp.float32
    )


def flat(h, c, y, l, z):
    return (h * 2 + c) * 32 + y * 8 + l * 4 + z


def perm(move):
    pairs = []
    for h in range(2):
        for c in range(2):
            for y in range(4):
                for l in range(2):
                    for z in range(4):
                        pairs.append((flat(h, c, y, l, z), flat(*move(h, c, y, l, z))))
    return pairs


STEP = {
    ("y", 1): perm(lambda h, c, y, l, z: (h, c, (y + 1) % 4, l, z)),
    ("y", -1): perm(lambda h, c, y, l, z: (h, c, (y - 1) % 4, l, z)),
    ("z", 1): perm(lambda h, c, y, l, z: (h, c, y, l, (z + 1) % 4)),
    ("z", -1): perm(lambda h, c, y, l, z: (h, c, y, l, (z - 1) % 4)),
}
TURN = {
    ("y", 1): perm(lambda h, c, y, l, z: (h, c, (y + 1 - 2 * c) % 4, l, z)),
    ("y", -1): perm(lambda h, c, y, l, z: (h, c, (y - 1 + 2 * c) % 4, l, z)),
    ("z", 1): perm(lambda h, c, y, l, z: (h, c, y, l, (z + 1 - 2 * c) % 4)),
    ("z", -1): perm(lambda h, c, y, l, z: (h, c, y, l, (z - 1 + 2 * c) % 4)),
}
PARTNER = perm(lambda h, c, y, l, z: (h, c, y, 1 - l, z))
CORE = perm(lambda h, c, y, l, z: (h, 1 - c, y, l, z))
ACROSS = perm(lambda h, c, y, l, z: (1 - h, c, y, l if c == 0 else 1 - l, z))
OTHER = perm(lambda h, c, y, l, z: (1 - h, c, y, l, z))
MIB = 1 << 20


def gram_kernel(slabs, layout, skip, gives, count, local, r0, r1, *refs):
    sources, refs = refs[:count], refs[count:]
    own_ref, sum_ref, refs = refs[0], refs[1], refs[2:]
    targets = [(r0, own_ref)]
    if gives:
        give_ref, acc, refs = refs[0], refs[1], refs[2:]
        targets.append((r1, acc))
        acc[...] = jnp.zeros_like(acc)
    xs, sems = refs[:-1], refs[-1]
    i = pl.program_id(0)
    size = r0.shape[1] // slabs
    loads = [pltpu.make_async_copy(sources[n], xs[n], sems.at[n]) for n in range(count)]

    @pl.when(i == 0)
    def _():
        for load in loads:
            load.start()

    own_ref[...] = jnp.zeros_like(own_ref)
    seen = set()
    for k, ((a, ha), (b, hb)) in enumerate(layout):
        fresh = sorted({a, b} - seen)
        seen.update(fresh)

        @pl.when(i == k)
        def _(k=k, fresh=fresh, a=xs[a], ha=ha, b=xs[b], hb=hb):
            for n in fresh:
                loads[n].wait()
            for t in range(slabs):
                part = pl.ds(t * size, size)
                x = jnp.concatenate(
                    [a[pl.ds(128 * ha, 128), part], b[pl.ds(128 * hb, 128), part]], axis=0
                )
                for left, to in targets if k < 4 else targets[:1]:
                    to[local[t]] += lax.dot_general(
                        left[:, part],
                        x,
                        (((1,), (1,)), ((), ())),
                        preferred_element_type=jnp.float32,
                    )

    sum_ref[0] = own_ref[0] + own_ref[1]
    if gives:
        sum_ref[1] = acc[0] + acc[1]

        @pl.when((i >= skip) & (i < 4))
        def _():
            give_ref[...] = acc[...].astype(jnp.bfloat16)


def gram(local, rooted, partner, xs, layout, skip, gives):
    rows, m = rooted.shape[1], len(layout)
    whole = lambda x: pl.BlockSpec(
        x.shape, lambda i, f: (0, 0), pipeline_mode=pl.Buffered(1)
    )
    last = 3 - skip
    rank = 2 if gives else 1
    out_specs = [
        pl.BlockSpec((2, 256, 256), lambda i, f: (0, 0, i)),
        pl.BlockSpec((rank, 256, 256), lambda i, f: (0, 0, i)),
    ]
    out_shape = [
        pltpu.HBM((2, 256, 256 * m), jnp.float32),
        pltpu.HBM((rank, 256, 256 * m), jnp.float32),
    ]
    if gives:
        out_specs.append(
            pl.BlockSpec((2, 256, 256), lambda i, f: (0, 0, jnp.clip(i - skip, 0, last)))
        )
        out_shape.append(pltpu.HBM((2, 256, 256 * (last + 1)), jnp.bfloat16))
    return pl.pallas_call(
        lambda *refs: gram_kernel(local.shape[0], layout, skip, gives, len(xs), *refs),
        grid_spec=pltpu.PrefetchScalarGridSpec(
            num_scalar_prefetch=1,
            grid=(m,),
            in_specs=[whole(rooted), whole(partner)]
            + [pl.BlockSpec(memory_space=pl.ANY)] * len(xs),
            out_specs=out_specs,
            scratch_shapes=([pltpu.VMEM((2, 256, 256), jnp.float32)] if gives else [])
            + [pltpu.VMEM(x.shape, x.dtype) for x in xs]
            + [pltpu.SemaphoreType.DMA((len(xs),))],
        ),
        out_shape=out_shape,
        compiler_params=pltpu.CompilerParams(vmem_limit_bytes=20 * MIB),
        cost_estimate=pl.CostEstimate(
            flops=2 * 512 * 256 * m * rows, bytes_accessed=3 * m * MIB, transcendentals=0
        ),
    )(local, rooted, partner, *xs)


def stay(x):
    return pltpu.with_memory_space_constraint(x, pltpu.HBM)


def mix_kernel(r_ref, mine, theirs, *refs):
    refs[-1][...] = (mine[0] + theirs[0]).astype(jnp.bfloat16)


def mix(pick, s, swapped, half, parts, u):
    extra = [] if u is None else [u]
    base = 2 * half
    return pl.pallas_call(
        mix_kernel,
        grid_spec=pltpu.PrefetchScalarGridSpec(
            num_scalar_prefetch=1,
            grid=(2,),
            in_specs=[
                pl.BlockSpec((1, 256, 512), lambda i, r: (r[0], 0, i)),
                pl.BlockSpec((1, 256, 512), lambda i, r: (r[0], 0, i)),
            ]
            + [pl.BlockSpec(memory_space=pl.ANY)] * len(extra),
            out_specs=pl.BlockSpec((256, 512), lambda i, r: (0, i + base)),
        ),
        out_shape=pltpu.HBM((256, 1024 * parts), jnp.bfloat16),
        input_output_aliases={3: 0} if extra else {},
        compiler_params=pltpu.CompilerParams(vmem_limit_bytes=8 * MIB),
        cost_estimate=pl.CostEstimate(flops=MIB, bytes_accessed=3 * MIB, transcendentals=0),
    )(pick, stay(s), swapped, *extra)


def final_kernel(diagonal, skip, pick, cols, g0, s0, mine, theirs, dr, er, *refs):
    out, buf, sems = refs[-3:]
    n = pl.program_id(0)
    slot = lax.rem(n, 2)
    swap = pick[0] == 0

    def copies(step, slot):
        return [
            pltpu.make_async_copy(
                buf.at[slot, j, :, :, pl.ds(128 * k, 128)],
                out.at[:, :, pl.ds(pl.multiple_of(cols[4 * step + 2 * k + j] * 128, 128), 128)],
                sems.at[slot, j, k],
            )
            for j in range(2)
            for k in range(2)
        ]

    @pl.when(n >= 2)
    def _():
        for copy in copies(n - 2, slot):
            copy.wait()

    a, b = mine[...].astype(jnp.float32), theirs[...].astype(jnp.float32)
    rest = s0[0] + jnp.where(swap, a, b)
    if diagonal:
        rest = rest + jnp.where(n == 0, refs[2][...], 0.0)
    buf[slot, 0, 0] = g0[1] + rest
    buf[slot, 0, 1] = g0[0] + rest
    rest = jnp.where(swap, b, a)
    if skip:

        @pl.when(n < skip)
        def _():
            gp, sp = refs[0], refs[1]
            buf[slot, 1, 0] = gp[1] + sp[0] + rest
            buf[slot, 1, 1] = gp[0] + sp[0] + rest

    @pl.when(n >= skip)
    def _():
        other = er[0].astype(jnp.float32) + er[1].astype(jnp.float32) + rest
        buf[slot, 1, 0] = dr[1].astype(jnp.float32) + other
        buf[slot, 1, 1] = dr[0].astype(jnp.float32) + other

    for copy in copies(n, slot):
        copy.start()

    @pl.when(n == 3)
    def _():
        for step in (2, 3):
            for copy in copies(step, step % 2):
                copy.wait()


def final(pick, cols, g, swapped, mine, theirs, half, dr, er, skip, known, pen, out, total):
    base = 4 * half
    extra, extra_specs, alias = [], [], {}
    if skip:
        gp, sp, at = known
        extra += [stay(gp), sp]
        extra_specs += [
            pl.BlockSpec((2, 256, 256), lambda n, p, c: (0, 0, at + jnp.minimum(n, skip - 1))),
            pl.BlockSpec((1, 256, 256), lambda n, p, c: (0, 0, at + jnp.minimum(n, skip - 1))),
        ]
    if out is None:
        extra.append(pen)
        extra_specs.append(pl.BlockSpec((256, 256), lambda n, p, c: (0, 0)))
    else:
        alias = {8 + len(extra): 0}
        extra.append(out)
        extra_specs.append(pl.BlockSpec(memory_space=pl.ANY))
    return pl.pallas_call(
        lambda *refs: final_kernel(out is None, skip, *refs),
        grid_spec=pltpu.PrefetchScalarGridSpec(
            num_scalar_prefetch=2,
            grid=(4,),
            in_specs=[
                pl.BlockSpec((2, 256, 256), lambda n, p, c: (0, 0, n)),
                pl.BlockSpec((1, 256, 256), lambda n, p, c: (0, 0, n)),
                pl.BlockSpec((256, 256), lambda n, p, c: (0, n + base)),
                pl.BlockSpec((256, 256), lambda n, p, c: (0, n + base)),
            ]
            + [pl.BlockSpec((2, 256, 256), lambda n, p, c: (0, 0, jnp.maximum(n - skip, 0)))] * 2
            + extra_specs,
            out_specs=pl.BlockSpec(memory_space=pl.ANY),
            scratch_shapes=[
                pltpu.VMEM((2, 2, 2, 256, 256), jnp.float32),
                pltpu.SemaphoreType.DMA((2, 2, 2)),
            ],
        ),
        out_shape=pltpu.HBM((2, 256, total), jnp.float32),
        input_output_aliases=alias,
        compiler_params=pltpu.CompilerParams(vmem_limit_bytes=12 * MIB),
        cost_estimate=pl.CostEstimate(flops=MIB, bytes_accessed=9 * MIB, transcendentals=0),
    )(pick, cols, stay(g), swapped, mine, theirs, dr, er, *extra)


def body(design, weights, response, fold_of, smoothing):
    rows, block = design.shape
    slabs = fold_of.shape[0]
    width = block * 32
    fold, tile = lax.axis_index("fold"), lax.axis_index("tile")
    core = lax.rem(fold, 2)
    me_y, me_l, me_z = tile // 8, lax.rem(tile // 4, 2), lax.rem(tile, 4)
    pick = core.reshape(1).astype(jnp.int32)
    local = fold_of - 2 * fold

    def send(x, pairs):
        return lax.ppermute(x, AXES, pairs)

    root_w = jnp.sqrt(weights)
    rooted = (design.astype(jnp.float32) * root_w[:, None]).astype(jnp.bfloat16).T
    rooted = lax.optimization_barrier(rooted)
    partner = send(rooted, PARTNER)

    target = root_w * response
    member = jnp.repeat(local, rows // slabs)
    prod = rooted.astype(jnp.float32) * target[None, :]
    rhs = jnp.stack([jnp.sum(jnp.where(member == f, prod, 0.0), axis=1) for f in range(2)])
    chip_rhs = jnp.sum(rhs, axis=0)
    chip_rhs = chip_rhs + send(chip_rhs, CORE)
    total_rhs = chip_rhs + send(chip_rhs, OTHER)
    complement_rhs = total_rhs[None] - rhs

    blocks = ([rooted], [], [], [])
    where = ([(0, 0, 0), (0, 0, 1)], [], [], [])
    far = []
    for colour, (p, q) in enumerate((("y", "z"), ("z", "y"))):
        at = lambda u, v, p=p, k=colour: (u, v, k) if p == "y" else (v, u, k)
        own = rooted[128 * colour : 128 * (colour + 1)]
        a = send(own, TURN[p, 1])
        b = send(own, TURN[p, -1])
        d = send(a, TURN[p, 1])
        ab = jnp.concatenate([jnp.where(core == 0, a, b), jnp.where(core == 0, b, a)], axis=0)
        ab_m, ab_p = send(ab, STEP[q, 1]), send(ab, STEP[q, -1])
        od = jnp.concatenate([own, d], axis=0)
        od_m, od_p = send(od, STEP[q, 1]), send(od, STEP[q, -1])
        ab_2 = send(ab_m, STEP[q, 1])
        od_2 = send(od_p, STEP[q, -1])
        blocks[0].append(ab)
        far.append(d)
        blocks[1].extend([ab_m, ab_p])
        blocks[2].extend([od_m, od_p])
        blocks[3].extend([ab_2, od_2])
        where[0].extend(at(o, 0) for o in (-1, 1))
        where[1].extend(at(o, v) for v in (-1, 1) for o in (-1, 1))
        where[2].extend(at(0, v) for v in (-1, 1))
        where[3].extend(at(o, 2) for o in (-1, 1, 0, 2))
    where[0].extend([(2, 0, 0), (0, 2, 1)])
    where[2].extend([(2, -1, 0), (2, 1, 0), (-1, 2, 1), (1, 2, 1)])
    blocks[0].extend(far + [partner])
    both = lambda k: ((k, 0), (k, 1))
    layouts = (
        (both(0), both(1), both(2), ((3, 0), (4, 0)), both(5)),
        tuple(both(k) for k in range(4)),
        tuple(((k, half), (k + 1, half)) for half in range(2) for k in (0, 2)),
        tuple(both(k) for k in range(4)),
    )
    skips = (1, 0, 2, 0)

    pen = jnp.kron(jnp.diag(smoothing), second_differences(TERM))
    halves = (partner[:128], partner[128:])
    local, pen, halves = lax.optimization_barrier((local, pen, halves))

    places = ((0, 0, 1), (1, 0, 1), (2, 0, 1), (3, 0, 1))
    state, mine, theirs, u = [], [], [], None
    for n, xs in enumerate(blocks):
        if n == 2:
            local, complement_rhs = lax.optimization_barrier((local, complement_rhs))
        message, half, parts = places[n]
        g, s, give = gram(local, rooted, partner, xs, layouts[n], skips[n], True)
        swapped = send(s, CORE)
        dr = send(give, PARTNER)
        er = send(dr, CORE)
        u = mix(pick, s, swapped, half, parts, u)
        state.append((g, swapped, dr, er))
        if half == parts - 1:
            mine.append(send(u, ACROSS))
            theirs.append(send(mine[-1], CORE))
            u = None
    known = []
    for colour, q in enumerate("zy"):
        known.append(send(halves[colour], STEP[q, 1]))
        known.append(send(halves[colour], STEP[q, -1]))
    pair = lambda k: ((k, 0), (k + 1, 0))
    g_known, s = gram(local, rooted, partner, known, (pair(0), pair(2)), 0, False)
    s_known = send(s, CORE)
    raw = {0: (state[0][0], state[0][1], 4), 2: (g_known, s_known, 0)}
    out = None
    for n, (g, swapped, dr, er) in enumerate(state):
        message, half, _ = places[n]
        cols = []
        for dy, dz, colour in where[n]:
            y, z = lax.rem(me_y + dy + 4, 4), lax.rem(me_z + dz + 4, 4)
            for l in (me_l, 1 - me_l):
                cols.append((y * 8 + l * 4 + z) * 2 + colour)
        cols = jnp.stack(cols).astype(jnp.int32)
        v0, v1 = mine[message], theirs[message]
        out = final(
            pick, cols, g, swapped, v0, v1, half, dr, er, skips[n], raw.get(n), pen, out, width
        )
    return (out, complement_rhs)


def solution(mesh):
    in_specs = (P("fold", "tile"), P("fold"), P("fold"), P("fold"), P("tile"))
    out_specs = (P("fold", "tile", None), P("fold", "tile"))

    return jax.shard_map(body, mesh=mesh, in_specs=in_specs, out_specs=out_specs, check_vma=False)
```

```python
import jax
import jax.numpy as jnp
from jax import lax
from jax.experimental import pallas as pl
from jax.experimental.pallas import tpu as pltpu
from jax.sharding import PartitionSpec as P


TERM = 64
AXES = ("fold", "tile")


def second_differences(width):
    rows = lax.broadcasted_iota(jnp.int32, (width - 2, width), 0)
    cols = lax.broadcasted_iota(jnp.int32, (width - 2, width), 1)
    diffs = (
        jnp.where(cols == rows, 1.0, 0.0)
        + jnp.where(cols == rows + 1, -2.0, 0.0)
        + jnp.where(cols == rows + 2, 1.0, 0.0)
    )
    diffs = diffs.astype(jnp.float32)
    return jnp.dot(
        diffs.T, diffs, precision=lax.Precision.HIGHEST, preferred_element_type=jnp.float32
    )


def flat(h, c, y, l, z):
    return (h * 2 + c) * 32 + y * 8 + l * 4 + z


def perm(move):
    pairs = []
    for h in range(2):
        for c in range(2):
            for y in range(4):
                for l in range(2):
                    for z in range(4):
                        pairs.append((flat(h, c, y, l, z), flat(*move(h, c, y, l, z))))
    return pairs


def even(v):
    return v + 1 - 2 * (v % 2)


def odd(v):
    return (v - 1 + 2 * (v % 2)) % 4


STEP = {
    ("y", 1): perm(lambda h, c, y, l, z: (h, c, even(y), l, z)),
    ("y", -1): perm(lambda h, c, y, l, z: (h, c, odd(y), l, z)),
    ("z", 1): perm(lambda h, c, y, l, z: (h, c, y, l, even(z))),
    ("z", -1): perm(lambda h, c, y, l, z: (h, c, y, l, odd(z))),
}
TURN = {
    ("y", 1): perm(lambda h, c, y, l, z: (h, c, (y + 1 - 2 * c) % 4, l, z)),
    ("y", -1): perm(lambda h, c, y, l, z: (h, c, (y - 1 + 2 * c) % 4, l, z)),
    ("z", 1): perm(lambda h, c, y, l, z: (h, c, y, l, (z + 1 - 2 * c) % 4)),
    ("z", -1): perm(lambda h, c, y, l, z: (h, c, y, l, (z - 1 + 2 * c) % 4)),
}
PARTNER = perm(lambda h, c, y, l, z: (h, c, y, 1 - l, z))
CORE = perm(lambda h, c, y, l, z: (h, 1 - c, y, l, z))
ACROSS = perm(lambda h, c, y, l, z: (1 - h, c, y, l if c == 0 else 1 - l, z))
OTHER = perm(lambda h, c, y, l, z: (1 - h, c, y, l, z))
MIB = 1 << 20


def gram_kernel(slabs, layout, skip, gives, count, local, r0, r1, *refs):
    sources, refs = refs[:count], refs[count:]
    own_ref, sum_ref, refs = refs[0], refs[1], refs[2:]
    targets = [(r0, own_ref)]
    if gives:
        give_ref, acc, refs = refs[0], refs[1], refs[2:]
        targets.append((r1, acc))
        acc[...] = jnp.zeros_like(acc)
    xs, sems = refs[:-1], refs[-1]
    i = pl.program_id(0)
    size = r0.shape[1] // slabs
    loads = [pltpu.make_async_copy(sources[n], xs[n], sems.at[n]) for n in range(count)]

    @pl.when(i == 0)
    def _():
        for load in loads:
            load.start()

    own_ref[...] = jnp.zeros_like(own_ref)
    seen = set()
    for k, ((a, ha), (b, hb)) in enumerate(layout):
        fresh = sorted({a, b} - seen)
        seen.update(fresh)

        @pl.when(i == k)
        def _(k=k, fresh=fresh, a=xs[a], ha=ha, b=xs[b], hb=hb):
            for n in fresh:
                loads[n].wait()
            for t in range(slabs):
                part = pl.ds(t * size, size)
                x = jnp.concatenate(
                    [a[pl.ds(128 * ha, 128), part], b[pl.ds(128 * hb, 128), part]], axis=0
                )
                for left, to in targets if k < 4 else targets[:1]:
                    to[local[t]] += lax.dot_general(
                        left[:, part],
                        x,
                        (((1,), (1,)), ((), ())),
                        preferred_element_type=jnp.float32,
                    )

    sum_ref[0] = own_ref[0] + own_ref[1]
    if gives:
        sum_ref[1] = acc[0] + acc[1]

        @pl.when((i >= skip) & (i < 4))
        def _():
            give_ref[...] = acc[...].astype(jnp.bfloat16)


def gram(local, rooted, partner, xs, layout, skip, gives):
    rows, m = rooted.shape[1], len(layout)
    whole = lambda x: pl.BlockSpec(
        x.shape, lambda i, f: (0, 0), pipeline_mode=pl.Buffered(1)
    )
    last = 3 - skip
    rank = 2 if gives else 1
    out_specs = [
        pl.BlockSpec((2, 256, 256), lambda i, f: (0, 0, i)),
        pl.BlockSpec((rank, 256, 256), lambda i, f: (0, 0, i)),
    ]
    out_shape = [
        pltpu.HBM((2, 256, 256 * m), jnp.float32),
        pltpu.HBM((rank, 256, 256 * m), jnp.float32),
    ]
    if gives:
        out_specs.append(
            pl.BlockSpec((2, 256, 256), lambda i, f: (0, 0, jnp.clip(i - skip, 0, last)))
        )
        out_shape.append(pltpu.HBM((2, 256, 256 * (last + 1)), jnp.bfloat16))
    return pl.pallas_call(
        lambda *refs: gram_kernel(local.shape[0], layout, skip, gives, len(xs), *refs),
        grid_spec=pltpu.PrefetchScalarGridSpec(
            num_scalar_prefetch=1,
            grid=(m,),
            in_specs=[whole(rooted), whole(partner)]
            + [pl.BlockSpec(memory_space=pl.ANY)] * len(xs),
            out_specs=out_specs,
            scratch_shapes=([pltpu.VMEM((2, 256, 256), jnp.float32)] if gives else [])
            + [pltpu.VMEM(x.shape, x.dtype) for x in xs]
            + [pltpu.SemaphoreType.DMA((len(xs),))],
        ),
        out_shape=out_shape,
        compiler_params=pltpu.CompilerParams(vmem_limit_bytes=20 * MIB),
        cost_estimate=pl.CostEstimate(
            flops=2 * 512 * 256 * m * rows, bytes_accessed=3 * m * MIB, transcendentals=0
        ),
    )(local, rooted, partner, *xs)


def stay(x):
    return pltpu.with_memory_space_constraint(x, pltpu.HBM)


def mix_kernel(r_ref, mine, theirs, *refs):
    refs[-1][...] = (mine[0] + theirs[0]).astype(jnp.bfloat16)


def mix(pick, s, swapped, half, parts, u):
    extra = [] if u is None else [u]
    base = 2 * half
    return pl.pallas_call(
        mix_kernel,
        grid_spec=pltpu.PrefetchScalarGridSpec(
            num_scalar_prefetch=1,
            grid=(2,),
            in_specs=[
                pl.BlockSpec((1, 256, 512), lambda i, r: (r[0], 0, i)),
                pl.BlockSpec((1, 256, 512), lambda i, r: (r[0], 0, i)),
            ]
            + [pl.BlockSpec(memory_space=pl.ANY)] * len(extra),
            out_specs=pl.BlockSpec((256, 512), lambda i, r: (0, i + base)),
        ),
        out_shape=pltpu.HBM((256, 1024 * parts), jnp.bfloat16),
        input_output_aliases={3: 0} if extra else {},
        compiler_params=pltpu.CompilerParams(vmem_limit_bytes=8 * MIB),
        cost_estimate=pl.CostEstimate(flops=MIB, bytes_accessed=3 * MIB, transcendentals=0),
    )(pick, stay(s), swapped, *extra)


def final_kernel(diagonal, skip, pick, cols, g0, s0, mine, theirs, dr, er, *refs):
    out, buf, sems = refs[-3:]
    n = pl.program_id(0)
    slot = lax.rem(n, 2)
    swap = pick[0] == 0

    def copies(step, slot):
        return [
            pltpu.make_async_copy(
                buf.at[slot, j, :, :, pl.ds(128 * k, 128)],
                out.at[:, :, pl.ds(pl.multiple_of(cols[4 * step + 2 * k + j] * 128, 128), 128)],
                sems.at[slot, j, k],
            )
            for j in range(2)
            for k in range(2)
        ]

    @pl.when(n >= 2)
    def _():
        for copy in copies(n - 2, slot):
            copy.wait()

    a, b = mine[...].astype(jnp.float32), theirs[...].astype(jnp.float32)
    rest = s0[0] + jnp.where(swap, a, b)
    if diagonal:
        rest = rest + jnp.where(n == 0, refs[2][...], 0.0)
    buf[slot, 0, 0] = g0[1] + rest
    buf[slot, 0, 1] = g0[0] + rest
    rest = jnp.where(swap, b, a)
    if skip:

        @pl.when(n < skip)
        def _():
            gp, sp = refs[0], refs[1]
            buf[slot, 1, 0] = gp[1] + sp[0] + rest
            buf[slot, 1, 1] = gp[0] + sp[0] + rest

    @pl.when(n >= skip)
    def _():
        other = er[0].astype(jnp.float32) + er[1].astype(jnp.float32) + rest
        buf[slot, 1, 0] = dr[1].astype(jnp.float32) + other
        buf[slot, 1, 1] = dr[0].astype(jnp.float32) + other

    for copy in copies(n, slot):
        copy.start()

    @pl.when(n == 3)
    def _():
        for step in (2, 3):
            for copy in copies(step, step % 2):
                copy.wait()


def final(pick, cols, g, swapped, mine, theirs, half, dr, er, skip, known, pen, out, total):
    base = 4 * half
    extra, extra_specs, alias = [], [], {}
    if skip:
        gp, sp, at = known
        extra += [stay(gp), sp]
        extra_specs += [
            pl.BlockSpec((2, 256, 256), lambda n, p, c: (0, 0, at + jnp.minimum(n, skip - 1))),
            pl.BlockSpec((1, 256, 256), lambda n, p, c: (0, 0, at + jnp.minimum(n, skip - 1))),
        ]
    if out is None:
        extra.append(pen)
        extra_specs.append(pl.BlockSpec((256, 256), lambda n, p, c: (0, 0)))
    else:
        alias = {8 + len(extra): 0}
        extra.append(out)
        extra_specs.append(pl.BlockSpec(memory_space=pl.ANY))
    return pl.pallas_call(
        lambda *refs: final_kernel(out is None, skip, *refs),
        grid_spec=pltpu.PrefetchScalarGridSpec(
            num_scalar_prefetch=2,
            grid=(4,),
            in_specs=[
                pl.BlockSpec((2, 256, 256), lambda n, p, c: (0, 0, n)),
                pl.BlockSpec((1, 256, 256), lambda n, p, c: (0, 0, n)),
                pl.BlockSpec((256, 256), lambda n, p, c: (0, n + base)),
                pl.BlockSpec((256, 256), lambda n, p, c: (0, n + base)),
            ]
            + [pl.BlockSpec((2, 256, 256), lambda n, p, c: (0, 0, jnp.maximum(n - skip, 0)))] * 2
            + extra_specs,
            out_specs=pl.BlockSpec(memory_space=pl.ANY),
            scratch_shapes=[
                pltpu.VMEM((2, 2, 2, 256, 256), jnp.float32),
                pltpu.SemaphoreType.DMA((2, 2, 2)),
            ],
        ),
        out_shape=pltpu.HBM((2, 256, total), jnp.float32),
        input_output_aliases=alias,
        compiler_params=pltpu.CompilerParams(vmem_limit_bytes=12 * MIB),
        cost_estimate=pl.CostEstimate(flops=MIB, bytes_accessed=9 * MIB, transcendentals=0),
    )(pick, cols, stay(g), swapped, mine, theirs, dr, er, *extra)


def body(design, weights, response, fold_of, smoothing):
    rows, block = design.shape
    slabs = fold_of.shape[0]
    width = block * 32
    fold, tile = lax.axis_index("fold"), lax.axis_index("tile")
    core = lax.rem(fold, 2)
    me_y, me_l, me_z = tile // 8, lax.rem(tile // 4, 2), lax.rem(tile, 4)
    pick = core.reshape(1).astype(jnp.int32)
    local = fold_of - 2 * fold

    def send(x, pairs):
        return lax.ppermute(x, AXES, pairs)

    root_w = jnp.sqrt(weights)
    rooted = (design.astype(jnp.float32) * root_w[:, None]).astype(jnp.bfloat16).T
    rooted = lax.optimization_barrier(rooted)
    partner = send(rooted, PARTNER)

    target = root_w * response
    member = jnp.repeat(local, rows // slabs)
    prod = rooted.astype(jnp.float32) * target[None, :]
    rhs = jnp.stack([jnp.sum(jnp.where(member == f, prod, 0.0), axis=1) for f in range(2)])
    chip_rhs = jnp.sum(rhs, axis=0)
    chip_rhs = chip_rhs + send(chip_rhs, CORE)
    total_rhs = chip_rhs + send(chip_rhs, OTHER)
    complement_rhs = total_rhs[None] - rhs

    blocks = ([rooted], [], [], [])
    where = ([(0, 0, 0), (0, 0, 1)], [], [], [])
    far = []
    for colour, (p, q) in enumerate((("y", "z"), ("z", "y"))):
        at = lambda u, v, p=p, k=colour: (u, v, k) if p == "y" else (v, u, k)
        own = rooted[128 * colour : 128 * (colour + 1)]
        a = send(own, TURN[p, 1])
        b = send(own, TURN[p, -1])
        d = send(a, TURN[p, 1])
        ab = jnp.concatenate([jnp.where(core == 0, a, b), jnp.where(core == 0, b, a)], axis=0)
        ab_m, ab_p = send(ab, STEP[q, 1]), send(ab, STEP[q, -1])
        od = jnp.concatenate([own, d], axis=0)
        od_m, od_p = send(od, STEP[q, 1]), send(od, STEP[q, -1])
        ab_2 = send(ab_m, STEP[q, -1])
        od_2 = send(od_p, STEP[q, 1])
        blocks[0].append(ab)
        far.append(d)
        blocks[1].extend([ab_m, ab_p])
        blocks[2].extend([od_m, od_p])
        blocks[3].extend([ab_2, od_2])
        where[0].extend(at(o, 0) for o in (-1, 1))
        where[1].extend(at(o, v) for v in (1, -1) for o in (-1, 1))
        where[2].extend(at(0, v) for v in (1, -1))
        where[3].extend(at(o, 2) for o in (-1, 1, 0, 2))
    where[0].extend([(2, 0, 0), (0, 2, 1)])
    where[2].extend([(2, 1, 0), (2, -1, 0), (1, 2, 1), (-1, 2, 1)])
    blocks[0].extend(far + [partner])
    both = lambda k: ((k, 0), (k, 1))
    layouts = (
        (both(0), both(1), both(2), ((3, 0), (4, 0)), both(5)),
        tuple(both(k) for k in range(4)),
        tuple(((k, half), (k + 1, half)) for half in range(2) for k in (0, 2)),
        tuple(both(k) for k in range(4)),
    )
    skips = (1, 0, 2, 0)

    pen = jnp.kron(jnp.diag(smoothing), second_differences(TERM))
    halves = (partner[:128], partner[128:])
    local, pen, halves = lax.optimization_barrier((local, pen, halves))

    places = ((0, 0, 1), (1, 0, 1), (2, 0, 1), (3, 0, 1))
    state, mine, theirs, u = [], [], [], None
    for n, xs in enumerate(blocks):
        if n == 2:
            local, complement_rhs = lax.optimization_barrier((local, complement_rhs))
        message, half, parts = places[n]
        g, s, give = gram(local, rooted, partner, xs, layouts[n], skips[n], True)
        swapped = send(s, CORE)
        dr = send(give, PARTNER)
        er = send(dr, CORE)
        u = mix(pick, s, swapped, half, parts, u)
        state.append((g, swapped, dr, er))
        if half == parts - 1:
            mine.append(send(u, ACROSS))
            theirs.append(send(mine[-1], CORE))
            u = None
    known = []
    for colour, q in enumerate("zy"):
        known.append(send(halves[colour], STEP[q, 1]))
        known.append(send(halves[colour], STEP[q, -1]))
    pair = lambda k: ((k, 0), (k + 1, 0))
    g_known, s = gram(local, rooted, partner, known, (pair(0), pair(2)), 0, False)
    s_known = send(s, CORE)
    raw = {0: (state[0][0], state[0][1], 4), 2: (g_known, s_known, 0)}
    turn_y, turn_z = 1 - 2 * lax.rem(me_y, 2), 1 - 2 * lax.rem(me_z, 2)
    out = None
    for n, (g, swapped, dr, er) in enumerate(state):
        message, half, _ = places[n]
        cols = []
        for dy, dz, colour in where[n]:
            if colour == 0:
                dz = dz * turn_z
            else:
                dy = dy * turn_y
            y, z = lax.rem(me_y + dy + 4, 4), lax.rem(me_z + dz + 4, 4)
            for l in (me_l, 1 - me_l):
                cols.append((y * 8 + l * 4 + z) * 2 + colour)
        cols = jnp.stack(cols).astype(jnp.int32)
        v0, v1 = mine[message], theirs[message]
        out = final(
            pick, cols, g, swapped, v0, v1, half, dr, er, skips[n], raw.get(n), pen, out, width
        )
    return (out, complement_rhs)


def solution(mesh):
    in_specs = (P("fold", "tile"), P("fold"), P("fold"), P("fold"), P("tile"))
    out_specs = (P("fold", "tile", None), P("fold", "tile"))

    return jax.shard_map(body, mesh=mesh, in_specs=in_specs, out_specs=out_specs, check_vma=False)
```
